768 devices in a mesh: rows: 256 (over z_lo, y, x, core), rep: 3 (over z_hi).
Axes of the slice: x: 4, y: 8, z: 12 (z_hi: 3, z_lo: 4; z = z_hi * 4 + z_lo), core: 2. Of those that a mesh axis runs over, the one named last changes fastest.
Arguments:
- features: bfloat16 [32768, 256], P('rows'), may hold values from -6 to 6
- weight: bfloat16 [256, 256], replicated, may hold values from -0.375 to 0.375
- beta: float32 [1], replicated, may hold values from 1 to 4
- edge_bits: int32 [256, 16, 32768], P(None, None, 'rows'), may hold values from 0 to 255, as said below
Outputs:
- aggregated: bfloat16 [32768, 256], P('rows')
The draws below stay inside these ranges and needn't reach their ends.
Inputs may be any that keep to these rules, and one draw needn't show every extreme that they name: Only the low 8 bits of a word are used; bit c of word w of edge_bits[b, w, n] is set for n = b * 128 + 8 * w + c (self edges); the words of a block pair with no other edges hold only these bits or are zero.
All inputs are finite; a program needn't handle non-finite values.
Results may differ from the reference program's by a relative error of at most 0.0051.
Values may be sent and summed in bfloat16 or wider, within the bound.
A program may use at most 128 MiB of HBM per device.

```python
import jax
import jax.numpy as jnp
from jax import lax

F = 256
ROWS_DEV = 128
BLOCKS = 256
NODES = 32768
WORDS = 16


def draw_edge_bits(key, part):
    keys = jax.random.split(jax.random.fold_in(key, 7), 8)
    source_class = jax.random.randint(keys[0], (BLOCKS,), 0, 4, dtype=jnp.int32)
    target_class = jax.random.randint(keys[1], (BLOCKS,), 0, 4, dtype=jnp.int32)
    ticket = jax.random.randint(keys[2], (BLOCKS, BLOCKS), 0, 2 * BLOCKS, dtype=jnp.int32)
    limit = jnp.left_shift(jnp.int32(1), source_class[:, None] + target_class[None, :])
    block_ids = jnp.arange(BLOCKS, dtype=jnp.int32)
    live = (ticket < limit) | (block_ids[:, None] == block_ids[None, :])
    node_ids = jnp.arange(NODES, dtype=jnp.int32)
    node_block = node_ids // ROWS_DEV
    live_nodes = live[:, node_block]
    shape = (BLOCKS, WORDS, NODES)
    packed = jax.random.randint(keys[3], shape, 0, 256, dtype=jnp.int32)
    for index in range(4, 7):
        packed = packed & jax.random.randint(keys[index], shape, 0, 256, dtype=jnp.int32)
    packed = jnp.where(live_nodes[:, None, :], packed, 0)
    inside = node_ids % ROWS_DEV
    word_ids = jnp.arange(WORDS, dtype=jnp.int32)
    self_bit = jnp.left_shift(jnp.int32(1), inside % 8)
    hit = (block_ids[:, None, None] == node_block[None, None, :]) & (word_ids[None, :, None] == (inside // 8)[None, None, :])
    return packed | jnp.where(hit, self_bit[None, None, :], 0)


def steps_of(own_key, extent, pieces, least, high):
    def one(axis_at, parts):
        heights = jax.random.uniform(jax.random.fold_in(jax.random.fold_in(own_key, 6), axis_at), (parts,), jnp.float32, least / len(pieces), high / len(pieces))
        return jnp.repeat(jnp.exp(heights), extent[axis_at] // parts).reshape((-1,) + (1,) * (len(extent) - axis_at - 1))

    gain = one(*pieces[0])
    for cut in pieces[1:]:
        gain = gain * one(*cut)
    return gain


def gaussian(rng, dims, scale, most, cuts=(), kind=jnp.bfloat16):
    entries = scale * jax.random.normal(rng, dims, jnp.float32)
    if cuts:
        entries = entries * steps_of(rng, dims, cuts, -0.22, 0.18)
    return jnp.clip(entries, -most, most).astype(kind)


def setup_inputs(seed: int = 0) -> dict:
    key_of = jax.random.split(jax.random.key(seed), 5)
    features = gaussian(key_of[0], (NODES, F), 1.0, 6.0, ((0, 256),))
    weight = gaussian(key_of[1], (F, F), F ** -0.5, 0.375)
    beta = jnp.clip(jax.random.uniform(key_of[2], (1,), jnp.float32, 1.0, 4.0), 1.0, 4.0)
    edge_bits = draw_edge_bits(jax.random.fold_in(key_of[4], 71), 0)
    return dict(features=features, weight=weight, beta=beta, edge_bits=edge_bits)


def inverse_norms(values):
    widened = values.astype(jnp.float32)
    return lax.rsqrt(lax.optimization_barrier(jnp.sum(widened * widened, axis=1)) + 1e-06)

def unpack_flags(packed):
    offsets = jnp.arange(8, dtype=jnp.int32)
    edge_flags = jnp.right_shift(packed[:, None, :], offsets[None, :, None]) & 1
    return edge_flags.reshape(packed.shape[0] * 8, packed.shape[1])

def tile_terms(target_rows, target_scale, source_panel, source_scale, packed, temper):
    scores = lax.dot_general(source_panel, target_rows, (((1,), (1,)), ((), ())), preferred_element_type=jnp.float32)
    scores = scores * source_scale[:, None] * target_scale[None, :] * temper
    weights = jnp.where(unpack_flags(packed) == 1, jnp.exp(scores - temper), 0.0)
    totals = lax.optimization_barrier(jnp.sum(weights, axis=0))
    weighted = lax.dot_general(weights.astype(jnp.bfloat16), source_panel, (((0,), (0,)), ((), ())), preferred_element_type=jnp.float32)
    return (totals, weighted)

def reference(features, weight, beta, edge_bits):
    projected = jnp.dot(features, weight, preferred_element_type=jnp.float32).astype(jnp.bfloat16)
    row_scale = inverse_norms(projected)
    block_rows = projected.reshape(BLOCKS, ROWS_DEV, F)
    block_scale = row_scale.reshape(BLOCKS, ROWS_DEV)
    temper = beta[0]

    def row_block(target):
        target_rows = block_rows[target]
        target_scale = block_scale[target]
        target_bits = lax.dynamic_slice_in_dim(edge_bits, target * ROWS_DEV, ROWS_DEV, 2)

        def section(carry, source):
            packed = target_bits[source]

            def work(state):
                part_totals, part_weighted = tile_terms(target_rows, target_scale, block_rows[source], block_scale[source], packed, temper)
                return (state[0] + part_totals, state[1] + part_weighted)
            return (lax.cond(jnp.any(packed != 0), work, lambda state: state, carry), None)
        start = (jnp.zeros((ROWS_DEV,), jnp.float32), jnp.zeros((ROWS_DEV, F), jnp.float32))
        (totals, weighted), unused = lax.scan(section, start, jnp.arange(BLOCKS, dtype=jnp.int32))
        return (weighted / totals[:, None]).astype(jnp.bfloat16)
    result = lax.map(row_block, jnp.arange(BLOCKS, dtype=jnp.int32))
    return result.reshape(NODES, F)
```

```python
import functools
import math

import jax
import jax.numpy as jnp
from jax import lax
from jax.experimental import pallas as pl
from jax.experimental.pallas import tpu as pltpu
from jax.sharding import PartitionSpec as P

MESH = pl.DeviceIdType.MESH
NX, NY, NZ, REPS = 4, 8, 4, 3
ROWS, F = 128, 256
PART, STRIDE = 48, 40
COLUMN, UA, UB = 192, 80, 112
A_GROUPS = [divmod(i, 6) for i in range(UA // 8)]
B_GROUPS = [divmod(i, 6) for i in range(UA // 8, COLUMN // 8)]
LOG2E = math.log2(math.e)


def kernel(
    features, weight, beta, edges, out,
    feat_v, weight_v, own_p, sib_p, stage, targets_t, own_e, sib_e,
    column, ax, ay, by, bx, acc, total, part_in, tot_out, tot_in, red, red_tot,
    load_sem, edge_sem, z_send, z_recv, s_send, s_recv,
    ax_send, ax_recv, ay_send, ay_recv, by_send, by_recv, bx_send, bx_recv,
    r_send, r_recv,
):
    me = lax.axis_index("rows")
    rep = lax.axis_index("rep")
    core = lax.rem(me, 2)
    x = lax.rem(lax.div(me, 2), NX)
    y = lax.rem(lax.div(me, 2 * NX), NY)
    zl = lax.div(me, 2 * NX * NY)
    depth = NZ * REPS
    z = rep * NZ + zl

    def device(dx=0, dy=0, dz=0, on=core):
        there = lax.rem(z + dz + depth, depth)
        row = lax.rem(there, NZ)
        row = row * NY + lax.rem(y + dy + NY, NY)
        row = row * NX + lax.rem(x + dx + NX, NX)
        return (row * 2 + on, lax.div(there, NZ))

    sibling = device(on=1 - core)
    x_up, x_down, x_far = device(dx=1), device(dx=-1), device(dx=2)
    y_up, y_down = device(dy=1), device(dy=-1)
    z_up, z_down = device(dz=1), device(dz=-1)
    z_up2, z_down2 = device(dz=2), device(dz=-2)
    z_far = device(dz=2 - 4 * core)
    r_up, r_down = device(dz=NZ), device(dz=-NZ)

    barrier = pltpu.get_barrier_semaphore()
    greeted = (sibling, x_up, x_down, x_far, y_up, y_down, z_up, z_down, z_up2, z_down2, r_up, r_down)
    for other in greeted:
        pl.semaphore_signal(barrier, inc=1, device_id=other, device_id_type=MESH)

    loads = [
        pltpu.make_async_copy(features, feat_v, load_sem.at[0]),
        pltpu.make_async_copy(weight, weight_v, load_sem.at[1]),
    ]
    for load in loads:
        load.start()
    edge_load = pltpu.make_async_copy(edges.at[:, core], own_e, edge_sem)
    edge_load.start()
    for load in loads:
        load.wait()
    rows = jnp.dot(feat_v[...], weight_v[...], preferred_element_type=jnp.float32)
    rows = rows.astype(jnp.bfloat16)
    own_p[...] = rows
    for r in range(REPS):
        stage[r] = rows[r * STRIDE : r * STRIDE + PART]
    pl.semaphore_wait(barrier, len(greeted))

    def remote(src, dst, send, recv, to):
        return pltpu.make_async_remote_copy(
            src_ref=src, dst_ref=dst, send_sem=send, recv_sem=recv, device_id=to, device_id_type=MESH
        )

    own_rows = column.at[pl.ds(pl.multiple_of(zl * PART, 16), PART)]

    def z_copy(slot, to):
        return remote(stage.at[to[1]], own_rows, z_send.at[slot], z_recv.at[slot], to)

    z_copies = [z_copy(0, z_up), z_copy(1, z_down), z_copy(2, z_far)]
    for copy in z_copies:
        copy.start()
    p_copy = remote(own_p, sib_p, s_send.at[0], s_recv.at[0], sibling)
    p_copy.start()
    e_copy = remote(edges.at[:, 1 - core], sib_e, s_send.at[1], s_recv.at[1], sibling)
    e_copy.start()
    own_copy = pltpu.make_async_copy(stage.at[rep], own_rows, load_sem.at[0])
    own_copy.start()

    bits = jnp.left_shift(jnp.int32(1), lax.broadcasted_iota(jnp.int32, (8, ROWS), 0))
    first_bits = jnp.where(rep == 0, bits, 0)
    temper = beta[0]
    shift = temper * LOG2E
    acc[...] = jnp.zeros_like(acc)
    total[...] = jnp.zeros_like(total)
    by[3, 1] = jnp.zeros((UB, F), jnp.bfloat16)

    p_copy.wait_recv()
    both = jnp.concatenate([own_p[...].astype(jnp.float32), sib_p[...].astype(jnp.float32)], axis=0)
    turned = both.T
    targets_t[...] = turned.astype(jnp.bfloat16)
    squares = jnp.sum(turned * turned, axis=0, keepdims=True)
    target_scale = lax.rsqrt(squares + 1e-06) * shift

    def column_groups(groups, dx, dy, live=None):
        there_x = lax.rem(x + dx + NX, NX)
        there_y = lax.rem(y + dy + NY, NY)
        return [(zc, there_y, there_x, word, live) for zc, word in groups]

    def attend(panel, groups):
        raw = jnp.dot(panel, targets_t[...], preferred_element_type=jnp.float32)
        wide = panel.astype(jnp.float32)
        norms = lax.rsqrt(jnp.sum(wide * wide, axis=1, keepdims=True) + 1e-06)
        weights = jnp.exp2(raw * norms * target_scale - shift)
        flags = []
        for zc, there_y, there_x, word, live in groups:
            block = (zc * NY + there_y) * NX + there_x
            wanted = first_bits if word == 0 else bits
            if live is not None:
                wanted = jnp.where(live, wanted, 0)
            row = rep * (STRIDE // 8) + word
            mine = own_e[block, pl.ds(row, 1), :] & wanted
            other = sib_e[block, pl.ds(row, 1), :] & wanted
            flags.append(jnp.concatenate([mine, other], axis=1))
        weights = jnp.where(jnp.concatenate(flags, axis=0) != 0, weights, 0.0)
        total[...] += jnp.sum(weights.reshape(-1, 8, 2 * ROWS), axis=0)
        acc[...] += lax.dot_general(
            weights.astype(jnp.bfloat16), panel, (((0,), (0,)), ((), ())), preferred_element_type=jnp.float32
        )

    def z_landing(slot, frm):
        zc = lax.rem(frm + NZ, NZ)
        rows_in = column.at[pl.ds(pl.multiple_of(zc * PART, 16), PART)]
        return remote(rows_in, rows_in, z_send.at[slot], z_recv.at[slot], sibling)

    own_copy.wait()
    z_landing(0, zl - 1).wait_recv()
    z_landing(1, zl + 1).wait_recv()
    z_landing(2, zl + 2).wait_recv()

    col_a = column.at[pl.ds(0, UA)]
    col_b = column.at[pl.ds(UA, UB)]

    def ax_copy(slot, to, src=None):
        return remote(col_a, ax.at[slot], ax_send.at[slot], ax_recv.at[slot], to)

    def ay_copy(src, k, side):
        to = (y_up, y_down)[side]
        return remote(src, ay.at[k, side], ay_send.at[k, side], ay_recv.at[k, side], to)

    def by_copy(src, p, side, slot):
        to = (y_up, y_down)[side]
        return remote(src, by.at[p, slot], by_send.at[p, slot], by_recv.at[p, slot], to)

    def bx_copy(src, k, side):
        to = (x_up, x_down)[side]
        return remote(src, bx.at[k, side], bx_send.at[k, side], bx_recv.at[k, side], to)

    by_copy(col_b, 0, 0, 0).start()
    by_copy(col_b, 0, 1, 1).start()
    ax_copy(0, x_up).start()
    ax_copy(1, x_down).start()
    ax_copy(2, x_far).start()
    bx_copy(col_b, 0, 0).start()
    bx_copy(col_b, 0, 1).start()
    ay_copy(col_a, 0, 0).start()
    ay_copy(col_a, 0, 1).start()

    edge_load.wait()
    e_copy.wait_recv()
    attend(column[...], column_groups(A_GROUPS + B_GROUPS, 0, 0))

    for slot in range(3):
        ax_copy(slot, sibling).wait_recv()
        ay_copy(ax.at[slot], slot + 1, 0).start()
        ay_copy(ax.at[slot], slot + 1, 1).start()
    x_of = (-1, 1, 2)
    attend(
        ax[...].reshape(3 * UA, F),
        sum([column_groups(A_GROUPS, x_of[slot], 0) for slot in range(3)], []),
    )

    def step(k, carry):
        @pl.when(k < 4)
        def _():
            by_copy(col_b, k, 0, 0).wait_recv()

            @pl.when(k < 3)
            def _():
                by_copy(col_b, k, 1, 1).wait_recv()

            @pl.when(k < 2)
            def _():
                by_copy(by.at[k, 0], k + 1, 0, 0).start()
                by_copy(by.at[k, 1], k + 1, 1, 1).start()

            @pl.when(jnp.logical_and(k == 2, core == 0))
            def _():
                by_copy(by.at[2, 0], 3, 0, 0).start()

            @pl.when(jnp.logical_and(k == 2, core == 1))
            def _():
                by_copy(by.at[2, 1], 3, 1, 0).start()

            bx_copy(by.at[k, 0], 2 * k + 1, 0).start()
            bx_copy(by.at[k, 0], 2 * k + 1, 1).start()

            @pl.when(k < 3)
            def _():
                bx_copy(by.at[k, 1], 2 * k + 2, 0).start()
                bx_copy(by.at[k, 1], 2 * k + 2, 1).start()

            attend(
                by[k].reshape(2 * UB, F),
                column_groups(B_GROUPS, 0, -(k + 1)) + column_groups(B_GROUPS, 0, k + 1, k < 3),
            )

        ay_copy(col_a, k, 0).wait_recv()
        ay_copy(col_a, k, 1).wait_recv()

        @pl.when(k < 8)
        def _():
            ay_copy(ay.at[k, 0], k + 4, 0).start()
            ay_copy(ay.at[k, 1], k + 4, 1).start()

        @pl.when(jnp.logical_or(k == 8, k == 10))
        def _():
            ay_copy(ay.at[k, 0], 12 + lax.div(k - 8, 2), 0).start()

        @pl.when(jnp.logical_or(k == 9, k == 11))
        def _():
            ay_copy(ay.at[k, 1], 12 + lax.div(k - 8, 2), 1).start()

        far = k >= 12
        j0 = jnp.where(far, 2 * (k - 12), lax.rem(k, 4))
        j1 = jnp.where(far, 2 * (k - 12) + 1, lax.rem(k, 4))
        d = jnp.where(far, 4, 1 + lax.div(k, 4))

        def x_offset(j):
            return jnp.where(j == 0, 0, jnp.where(j == 1, -1, j - 1))

        attend(
            ay[k].reshape(2 * UA, F),
            column_groups(A_GROUPS, x_offset(j0), -d) + column_groups(A_GROUPS, x_offset(j1), d),
        )

        @pl.when(k < 12)
        def _():
            bx_copy(col_b, k, 0).wait_recv()
            bx_copy(col_b, k, 1).wait_recv()

            @pl.when(jnp.logical_and(k < 8, lax.rem(k, 2) == 0))
            def _():
                bx_copy(bx.at[k, 0], 8 + lax.div(k, 2), 0).start()

            @pl.when(jnp.logical_and(k < 8, lax.rem(k, 2) == 1))
            def _():
                bx_copy(bx.at[k, 1], 8 + lax.div(k, 2), 1).start()

            near = k < 8
            i0 = jnp.where(near, k, 2 * (k - 8))
            i1 = jnp.where(near, k, 2 * (k - 8) + 1)

            def y_offset(i):
                half = lax.div(i + 1, 2)
                return jnp.where(lax.rem(i, 2) == 1, -half, half)

            attend(
                bx[k].reshape(2 * UB, F),
                column_groups(B_GROUPS, jnp.where(near, -1, 2), y_offset(i0))
                + column_groups(B_GROUPS, jnp.where(near, 1, 2), y_offset(i1)),
            )

        return carry

    lax.fori_loop(0, 14, step, 0)

    tot = jnp.sum(total[...], axis=0, keepdims=True)
    tot_out[...] = jnp.broadcast_to(tot[:, ROWS:], (8, ROWS))
    fold = [
        remote(acc.at[pl.ds(ROWS, ROWS)], part_in, r_send.at[0], r_recv.at[0], sibling),
        remote(tot_out, tot_in, r_send.at[1], r_recv.at[1], sibling),
    ]
    for copy in fold:
        copy.start()
    for copy in fold:
        copy.wait_recv()
    red[rep] = (acc[pl.ds(0, ROWS)] + part_in[...]).astype(jnp.bfloat16)
    red_tot[rep] = tot[:, :ROWS] + tot_in[...]

    def share(slot, frm, to):
        return [
            remote(red.at[frm], red.at[frm], r_send.at[slot], r_recv.at[slot], to),
            remote(red_tot.at[frm], red_tot.at[frm], r_send.at[slot + 1], r_recv.at[slot + 1], to),
        ]

    shares = share(2, rep, r_up) + share(4, rep, r_down)
    for copy in shares:
        copy.start()
    for copy in share(2, lax.rem(rep + REPS - 1, REPS), r_up) + share(4, lax.rem(rep + 1, REPS), r_down):
        copy.wait_recv()
    sums = red[0].astype(jnp.float32) + red[1].astype(jnp.float32) + red[2].astype(jnp.float32)
    tots = red_tot[0] + red_tot[1] + red_tot[2]
    tall = jnp.broadcast_to(tots[0:1], (ROWS, ROWS)).T
    out[:, :ROWS] = (sums[:, :ROWS] / tall).astype(jnp.bfloat16)
    out[:, ROWS:] = (sums[:, ROWS:] / tall).astype(jnp.bfloat16)

    for copy in z_copies + [p_copy, e_copy] + fold + shares:
        copy.wait_send()
    for slot in range(3):
        ax_copy(slot, sibling).wait_send()

    def drain(k, carry):
        ay_copy(col_a, k, 0).wait_send()
        ay_copy(col_a, k, 1).wait_send()

        @pl.when(k < 12)
        def _():
            bx_copy(col_b, k, 0).wait_send()
            bx_copy(col_b, k, 1).wait_send()

        @pl.when(k < 4)
        def _():
            by_copy(col_b, k, 0, 0).wait_send()

        @pl.when(k < 3)
        def _():
            by_copy(col_b, k, 1, 1).wait_send()

        return carry

    lax.fori_loop(0, 14, drain, 0)


def on_device(features, weight, beta, edge_bits):
    edges = edge_bits.reshape(NX * NY * NZ, 2, 16, ROWS)
    anywhere = pl.BlockSpec(memory_space=pl.ANY)
    bf16, f32, i32 = jnp.bfloat16, jnp.float32, jnp.int32
    dma = pltpu.SemaphoreType.DMA
    return pl.pallas_call(
        kernel,
        out_shape=jax.ShapeDtypeStruct((ROWS, F), bf16),
        in_specs=[anywhere, anywhere, pl.BlockSpec(memory_space=pltpu.SMEM), anywhere],
        out_specs=pl.BlockSpec(memory_space=pltpu.VMEM),
        scratch_shapes=[
            pltpu.VMEM((ROWS, F), bf16),
            pltpu.VMEM((F, F), bf16),
            pltpu.VMEM((ROWS, F), bf16),
            pltpu.VMEM((ROWS, F), bf16),
            pltpu.VMEM((REPS, PART, F), bf16),
            pltpu.VMEM((F, 2 * ROWS), bf16),
            pltpu.VMEM((NX * NY * NZ, 16, ROWS), i32),
            pltpu.VMEM((NX * NY * NZ, 16, ROWS), i32),
            pltpu.VMEM((COLUMN, F), bf16),
            pltpu.VMEM((3, UA, F), bf16),
            pltpu.VMEM((14, 2, UA, F), bf16),
            pltpu.VMEM((4, 2, UB, F), bf16),
            pltpu.VMEM((12, 2, UB, F), bf16),
            pltpu.VMEM((2 * ROWS, F), f32),
            pltpu.VMEM((8, 2 * ROWS), f32),
            pltpu.VMEM((ROWS, F), f32),
            pltpu.VMEM((8, ROWS), f32),
            pltpu.VMEM((8, ROWS), f32),
            pltpu.VMEM((REPS, ROWS, F), bf16),
            pltpu.VMEM((REPS, 8, ROWS), f32),
            dma((2,)), dma, dma((3,)), dma((3,)), dma((2,)), dma((2,)),
            dma((3,)), dma((3,)), dma((14, 2)), dma((14, 2)), dma((4, 2)), dma((4, 2)), dma((12, 2)), dma((12, 2)),
            dma((6,)), dma((6,)),
        ],
        compiler_params=pltpu.CompilerParams(collective_id=0, has_side_effects=True),
    )(features, weight, beta, edges)


def solution(mesh):
    return jax.shard_map(
        on_device,
        mesh=mesh,
        in_specs=(P("rows", None), P(), P(), P(None, None, "rows")),
        out_specs=P("rows", None),
        check_vma=False,
    )
```
